256 devices in a mesh: leaf: 32 (over z, x), row: 4 (over y), col: 2 (over core).
Axes of the slice: x: 4, y: 4, z: 8, core: 2. Of those that a mesh axis runs over, the one named last changes fastest.
Arguments:
- leaf_rhs: bfloat16 [65536, 1024], P(('leaf', 'col'), 'row'), may hold values from -6 to 6
- leaf_inverse: bfloat16 [65536, 2048], P('leaf', 'col'), may hold values from -0.125 to 0.125
- leaf_below: bfloat16 [65536, 2048], P('leaf', 'col'), may hold values from -0.0625 to 0.0625
- leaf_rows: int32 [32, 16], P('leaf'), may hold values from 16 to 511, as said below
- sep_rhs: bfloat16 [65536, 1024], P(('leaf', 'col'), 'row'), may hold values from -6 to 6
- sep_inverse: bfloat16 [65536, 2048], P('leaf', 'col'), may hold values from -0.125 to 0.125
- sep_below: bfloat16 [32768, 2048], P('leaf', 'col'), may hold values from -0.0625 to 0.0625
- sep_rows: int32 [32, 8], P('leaf'), may hold values from 16 to 511, as said below
- sep_width: int32 [32], replicated, may hold values from 1024 to 2048, as said below
Outputs:
- leaf_solution: bfloat16 [65536, 1024], P(('leaf', 'col'), 'row')
- sep_solution: bfloat16 [65536, 1024], P(('leaf', 'col'), 'row')
The draws below stay inside these ranges and needn't reach their ends.
Inputs may be any that keep to these rules, and one draw needn't show every extreme that they name: `sep_width`: multiples of 128; slot 32 / 2 (the root) has 2048; entry 0 is not used. `leaf_rows`: row i holds 16 different block rows a * 16 + p of the ancestors a of subtree i, with p * 128 < sep_width[a]. `sep_rows`: row a, for a slot a below the root, holds 8 different block rows b * 16 + p of the slots b at higher levels on the path from a to the root, with p * 128 < sep_width[b]; rows 0 and 16 are not used.
All inputs are finite; a program needn't handle non-finite values.
Results may differ from the reference program's by a relative error of at most 0.0065.
Values sent between devices are 32-bit elements; how exact they have to be, the bound alone decides.
A program may use at most 128 MiB of HBM per device.

```python
import jax
import jax.numpy as jnp
from jax import lax

WSEP = 2048
WLEAF = 2048
PANEL = 128
RPAN = 8
RLEAF = 16
RHS = 1024
LEVELS = 5
N_LEAF = 32


def widths_of(key):
    base_key = jax.random.fold_in(key, 11)
    counts_now = jax.random.randint(base_key, (N_LEAF,), RPAN, WSEP // PANEL + 1)
    counts_now = counts_now.at[1].set(RPAN)
    counts_now = counts_now.at[N_LEAF - 1].set(WSEP // PANEL)
    counts_now = counts_now.at[N_LEAF // 2].set(WSEP // PANEL)
    return (counts_now * PANEL).astype(jnp.int32)


def pick_rows(key, node_idx, own_level, count_rows, salt):
    sep_panels = WSEP // PANEL
    widths = widths_of(key)
    level_idx = jnp.arange(1, LEVELS + 1, dtype=jnp.int32)
    span_all = 2 ** level_idx
    ancestor = node_idx[:, None] - node_idx[:, None] % span_all[None, :] + span_all[None, :] // 2
    live_panels = widths[ancestor] // PANEL
    panel_idx = jnp.arange(sep_panels, dtype=jnp.int32)
    panel_ids = ancestor[:, :, None] * sep_panels + panel_idx[None, None, :]
    valid = (panel_idx[None, None, :] < live_panels[:, :, None]) & (level_idx[None, :, None] > own_level[:, None, None])
    raw_scores = jax.random.randint(jax.random.fold_in(key, salt), (N_LEAF, LEVELS, sep_panels), 0, 2 ** 16)
    position = jnp.arange(LEVELS * sep_panels, dtype=jnp.int32).reshape(LEVELS, sep_panels)
    scores = raw_scores * (LEVELS * sep_panels) + position[None, :, :]
    first_level = level_idx[None, :, None] == 1
    forced_low = first_level & (panel_idx[None, None, :] == 0)
    forced_high = first_level & (panel_idx[None, None, :] == live_panels[:, :, None] - 1)
    scores = jnp.where(forced_low, -2, scores)
    scores = jnp.where(forced_high, -1, scores)
    scores = jnp.where(valid, scores, scores + 2 ** 28)
    flat_scores = scores.reshape(N_LEAF, LEVELS * sep_panels)
    flat_ids = panel_ids.reshape(N_LEAF, LEVELS * sep_panels)
    best_values, chosen = lax.top_k(-flat_scores, count_rows)
    return jnp.take_along_axis(flat_ids, chosen, axis=1).astype(jnp.int32)


def draw_sep_width(key, part):
    return widths_of(key)


def draw_leaf_rows(key, part):
    node_idx = jnp.arange(N_LEAF, dtype=jnp.int32)
    return pick_rows(key, node_idx, jnp.zeros((N_LEAF,), jnp.int32), RLEAF, 21)


def draw_sep_rows(key, part):
    node_idx = jnp.arange(N_LEAF, dtype=jnp.int32)
    depth_now = jnp.ones_like(node_idx)
    for bit_pos in range(1, LEVELS + 1):
        depth_now = depth_now + (node_idx % 2 ** bit_pos == 0).astype(jnp.int32)
    own_level = jnp.where((node_idx == 0) | (depth_now >= LEVELS), 0, depth_now)
    path_node = jnp.where(node_idx == N_LEAF // 2, N_LEAF - 1, node_idx).astype(jnp.int32)
    return pick_rows(key, path_node, own_level, RPAN, 37)


def levels(rng, extent, pieces, low, high):
    def one(dim, blocks):
        heights = jax.random.uniform(jax.random.fold_in(jax.random.fold_in(rng, 6), dim), (blocks,), jnp.float32, low / len(pieces), high / len(pieces))
        return jnp.repeat(jnp.exp(heights), extent[dim] // blocks).reshape((-1,) + (1,) * (len(extent) - dim - 1))

    gain = one(*pieces[0])
    for cut in pieces[1:]:
        gain = gain * one(*cut)
    return gain


def gaussian(stream_key, shape, scale, most, cuts=(), kind=jnp.bfloat16):
    factor_of = levels(stream_key, shape, cuts, -0.22, 0.18) if cuts else 1.0
    drawn = jax.random.normal(stream_key, shape, jnp.float32) * scale * factor_of
    return jnp.minimum(jnp.maximum(drawn, -most), most).astype(kind)


def setup_inputs(seed: int = 0) -> dict:
    splits = jax.random.split(jax.random.key(seed), 10)
    leaf_rhs = gaussian(splits[0], (N_LEAF * WLEAF, RHS), 1.0, 6.0, ((0, 64), (1, 4)))
    leaf_inverse = gaussian(splits[1], (N_LEAF * WLEAF, WLEAF), WLEAF ** -0.5, 0.125, ((0, 32), (1, 2)))
    leaf_below = gaussian(splits[2], (N_LEAF * RLEAF * PANEL, WLEAF), (4 * WLEAF) ** -0.5, 0.0625, ((0, 32), (1, 2)))
    leaf_rows = draw_leaf_rows(jax.random.fold_in(splits[9], 71), 0)
    sep_rhs = gaussian(splits[4], (N_LEAF * WSEP, RHS), 1.0, 6.0, ((0, 64), (1, 4)))
    sep_inverse = gaussian(splits[5], (N_LEAF * WSEP, WSEP), WSEP ** -0.5, 0.125, ((0, 32), (1, 2)))
    sep_below = gaussian(splits[6], (N_LEAF * RPAN * PANEL, WSEP), (4 * WSEP) ** -0.5, 0.0625, ((0, 32), (1, 2)))
    sep_rows = draw_sep_rows(jax.random.fold_in(splits[9], 71), 0)
    sep_width = draw_sep_width(jax.random.fold_in(splits[9], 71), 0)
    return dict(leaf_rhs=leaf_rhs, leaf_inverse=leaf_inverse, leaf_below=leaf_below, leaf_rows=leaf_rows, sep_rhs=sep_rhs, sep_inverse=sep_inverse, sep_below=sep_below, sep_rows=sep_rows, sep_width=sep_width)


def unit_lower(matrix):
    size_now = matrix.shape[0]
    return jnp.tril(matrix, -1) + jnp.eye(size_now, dtype=matrix.dtype)


def reference(leaf_rhs, leaf_inverse, leaf_below, leaf_rows, sep_rhs, sep_inverse, sep_below, sep_rows, sep_width):
    sep_panels = WSEP // PANEL
    leaf_height = RLEAF * PANEL
    sep_height = RPAN * PANEL
    pending = jnp.zeros((N_LEAF * sep_panels, PANEL, RHS), jnp.float32)
    leaf_parts = []
    for leaf_now in range(N_LEAF):
        right_side = leaf_rhs[leaf_now * WLEAF:(leaf_now + 1) * WLEAF]
        inverse = unit_lower(leaf_inverse[leaf_now * WLEAF:(leaf_now + 1) * WLEAF])
        solution = jnp.dot(inverse, right_side, preferred_element_type=jnp.float32).astype(jnp.bfloat16)
        leaf_parts.append(solution)
        below_now = leaf_below[leaf_now * leaf_height:(leaf_now + 1) * leaf_height]
        update = jnp.dot(below_now, solution, preferred_element_type=jnp.float32).reshape(RLEAF, PANEL, RHS)
        pending = pending.at[leaf_rows[leaf_now]].add(update)
    sep_parts = [jnp.zeros((WSEP, RHS), jnp.bfloat16) for slot_now in range(N_LEAF)]
    columns = jnp.arange(WSEP)
    for level_now in range(1, LEVELS + 1):
        span_now = 2 ** level_now
        for slot_now in range(span_now // 2, N_LEAF, span_now):
            block_now = pending[slot_now * sep_panels:(slot_now + 1) * sep_panels].reshape(WSEP, RHS)
            residual = (sep_rhs[slot_now * WSEP:(slot_now + 1) * WSEP].astype(jnp.float32) - block_now).astype(jnp.bfloat16)
            inverse = unit_lower(sep_inverse[slot_now * WSEP:(slot_now + 1) * WSEP])
            product = jnp.dot(inverse, residual, preferred_element_type=jnp.float32)
            solution = jnp.where(columns[:, None] < sep_width[slot_now], product, 0.0).astype(jnp.bfloat16)
            sep_parts[slot_now] = solution
            if level_now < LEVELS:
                below_now = sep_below[slot_now * sep_height:(slot_now + 1) * sep_height]
                update = jnp.dot(below_now, solution, preferred_element_type=jnp.float32).reshape(RPAN, PANEL, RHS)
                pending = pending.at[sep_rows[slot_now]].add(update)
    return jnp.concatenate(leaf_parts, 0), jnp.concatenate(sep_parts, 0)
```

```python
import jax
import jax.numpy as jnp
from jax import lax
from jax.experimental import pallas as pl
from jax.experimental.pallas import tpu as pltpu
from jax.sharding import PartitionSpec as P

MESH = pl.DeviceIdType.MESH
F32 = jnp.float32
BF16 = jnp.bfloat16
PAN = 128
TILE = 256
LANES = 128
NX = 4
NZ = 8


def mm(a, b):
    return jnp.dot(a, b, preferred_element_type=F32)


def unit_tile(block):
    rows = lax.broadcasted_iota(jnp.int32, block.shape, 0)
    cols = lax.broadcasted_iota(jnp.int32, block.shape, 1)
    kept = jnp.where(rows > cols, block.astype(F32), 0.0)
    return jnp.where(rows == cols, 1.0, kept).astype(BF16)


def kernel(
    lrows, srows, swidth, lrhs_h, linv_h, lbel_h, srhs_h, sinv_h, sbel_h,
    lout, sout,
    ll, lb, bl, sr, lf, bf, stage, precv,
    us, ul, ur, uo, v1a, v1b, v2r, v2p, v3, v4, w, qs, qr, g,
    pps, prx, dbuf, xloc, usend, urecv, srf, srs, res, yb, ysend, yrecv,
    tb, ts,
    hsem, p10s, p10r, uxs, uxr, aS, aR, bS, bR, v1S, v1R, f1S, f1R,
    v2S, v2R, f2S, f2R, zS, zR, v3S, v3R, v5S, v5R, v4S, v4R,
    qS, qR, gS, gR, pS, pR, rS, rR, yS, yR, tS, tR, tzS, tzR, lsem,
):
    l = lax.axis_index("leaf")
    row = lax.axis_index("row")
    c = lax.axis_index("col")
    x = lax.rem(l, NX)
    z = lax.div(l, NX)
    zm = lax.rem(z, 4)
    odd = lax.rem(x, 2) == 1
    level = jnp.where(
        odd, 1,
        jnp.where(
            x == 2, 2,
            jnp.where(
                lax.rem(z, 2) == 1, 3,
                jnp.where(zm == 2, 4, jnp.where(z == 4, 5, 0)),
            ),
        ),
    )

    def at(xx, zz):
        return (zz * NX + xx, row, c)

    right = at(lax.rem(x + 1, NX), z)
    left = at(lax.rem(x + NX - 1, NX), z)
    partner = (l, row, 1 - c)

    def rc(src, dst, ss, rs, dev):
        return pltpu.make_async_remote_copy(
            src_ref=src, dst_ref=dst, send_sem=ss, recv_sem=rs,
            device_id=dev, device_id_type=MESH,
        )

    bar = pltpu.get_barrier_semaphore()
    pl.semaphore_signal(bar, 1, device_id=partner, device_id_type=MESH)
    for d in range(1, NX):
        pl.semaphore_signal(bar, 1, device_id=at(lax.rem(x + d, NX), z), device_id_type=MESH)
    for d in range(1, NZ):
        pl.semaphore_signal(bar, 1, device_id=at(x, lax.rem(z + d, NZ)), device_id_type=MESH)

    half = pl.multiple_of(c * 1024, 1024)
    cp_rhs = pltpu.make_async_copy(lrhs_h, bl, hsem.at[0])
    cp_hi = pltpu.make_async_copy(linv_h.at[pl.ds(1024, 1024)], ll.at[pl.ds(1024, 1024)], hsem.at[1])
    cp_lo = pltpu.make_async_copy(linv_h.at[pl.ds(0, 1024)], ll.at[pl.ds(0, 1024)], hsem.at[2])
    cp_lb = pltpu.make_async_copy(lbel_h, lb, hsem.at[3])
    cp_sr = pltpu.make_async_copy(srhs_h, sr, hsem.at[4])
    cp_lf = pltpu.make_async_copy(sinv_h, lf.at[:, pl.ds(half, 1024)], hsem.at[5])
    cp_bf = pltpu.make_async_copy(sbel_h, bf.at[:, pl.ds(half, 1024)], hsem.at[6])
    for cp in (cp_rhs, cp_hi, cp_lo, cp_lb, cp_sr, cp_lf, cp_bf):
        cp.start()

    lane = lax.broadcasted_iota(jnp.int32, (8, 128), 1)
    sub = lax.broadcasted_iota(jnp.int32, (8, 128), 0)
    span = jnp.left_shift(1, lax.shift_right_logical(lane, 4) + 1)
    base = l - jnp.bitwise_and(l, span - 1) + lax.shift_right_logical(span, 1)
    target = base * 16 + jnp.bitwise_and(lane, 15)
    inv_leaf = jnp.full((8, 128), 16, jnp.int32)
    for j in range(16):
        inv_leaf = jnp.where(target == lrows[0, j], j, inv_leaf)
    inv_sep = jnp.full((8, 128), 8, jnp.int32)
    for j in range(8):
        inv_sep = jnp.where(target == srows[0, j], j, inv_sep)
    tb[l] = jnp.where(sub == 0, inv_leaf, inv_sep)

    zero_panel = jnp.zeros((PAN, LANES), F32)
    for ref in (us, ul, ur, uo):
        ref[16] = zero_panel
    for ref in (v1a, v1b, v2r, v2p):
        ref[8] = zero_panel
    for i in range(4):
        v3[i, 8] = zero_panel
    for i in range(2):
        v4[i, 8] = zero_panel

    cp_rhs.wait()
    cp_hi.wait()

    @pl.when(c == 0)
    def _():
        for i in range(4):
            pps[i] = mm(ll[1024 + i * TILE : 1024 + (i + 1) * TILE, :], bl[...])

    pl.semaphore_wait(bar, 1 + (NX - 1) + (NZ - 1))

    def p10(i):
        return rc(pps.at[i], prx.at[i], p10s.at[i], p10r.at[i], partner)

    @pl.when(c == 0)
    def _():
        for i in range(4):
            p10(i).start()

    cp_lo.wait()
    for i in range(4):
        rows = pl.ds(pl.multiple_of(c * 1024 + i * TILE, TILE), TILE)
        acc = mm(unit_tile(ll[rows, i * TILE : (i + 1) * TILE]), bl[i * TILE : (i + 1) * TILE, :])
        if i:
            acc = acc + mm(ll[rows, : i * TILE], bl[: i * TILE, :])
        dbuf[...] = acc

        @pl.when(c == 1)
        def _():
            p10(i).wait_recv()
            dbuf[...] += prx[i]

        xloc[i * TILE : (i + 1) * TILE, :] = dbuf[...].astype(BF16)
    lout[...] = xloc[...]

    cp_lb.wait()

    def ux(j):
        return rc(usend.at[j], urecv.at[j], uxs.at[j], uxr.at[j], partner)

    def send_a(j, way):
        dst = ul if way == 0 else ur
        pan = pl.ds(2 * j, 2)
        return rc(us.at[pan], dst.at[pan], aS.at[way, j], aR.at[way, j], right if way == 0 else left)

    @pl.loop(0, 9)
    def _(j):
        @pl.when(j < 8)
        def _():
            t = mm(lb[pl.ds(pl.multiple_of(j * TILE, TILE), TILE), :], xloc[...])
            lo = t[:, :LANES]
            hi = t[:, LANES:]
            first = c == 0
            us[pl.ds(2 * j, 2)] = jnp.where(first, lo, hi).reshape(2, PAN, LANES)
            usend[j] = jnp.where(first, hi, lo).reshape(2, PAN, LANES)
            ux(j).start()

        @pl.when(j > 0)
        def _():
            i = j - 1
            ux(i).wait_recv()
            us[pl.ds(2 * i, 2)] += urecv[i]
            send_a(i, 0).start()
            send_a(i, 1).start()

    def tx(d):
        return rc(tb.at[l], tb.at[l], tS.at[d - 1], tR.at[d - 1], at(lax.rem(x + d, NX), z))

    def tx_in(d):
        src = tb.at[z * NX + lax.rem(x + NX - d, NX)]
        return rc(src, src, tS.at[d - 1], tR.at[d - 1], partner)

    def tz(d):
        rows = tb.at[pl.ds(z * NX, NX)]
        return rc(rows, rows, tzS.at[d - 1], tzR.at[d - 1], at(x, lax.rem(z + d, NZ)))

    def tz_in(d):
        rows = tb.at[pl.ds(lax.rem(z + NZ - d, NZ) * NX, NX)]
        return rc(rows, rows, tzS.at[d - 1], tzR.at[d - 1], partner)

    for d in range(1, NX):
        tx(d).start()

    cp_sr.wait()
    srv = sr[...].astype(F32)
    first = c == 0
    srs[...] = jnp.where(first, srv[:, LANES:], srv[:, :LANES])

    def rx():
        return rc(srs, srf.at[pl.ds(half, 1024)], rS, rR, partner)

    rx().start()
    srf[pl.ds(half, 1024), :] = jnp.where(first, srv[:, :LANES], srv[:, LANES:])

    cp_lf.wait()
    cp_bf.wait()

    def px(j):
        return rc(stage.at[lax.rem(j, 4)], precv.at[j], pS.at[j], pR.at[j], partner)

    first_j = jnp.where(c == 0, 0, 4)
    last_in = jnp.where(c == 0, 4, 0)

    @pl.loop(0, 12)
    def _(j):
        @pl.when(j >= first_j)
        def _():
            @pl.when(j >= first_j + 4)
            def _():
                px(j - 4).wait_send()

            @pl.when(j < 8)
            def _():
                rows = pl.ds(pl.multiple_of(j * TILE, TILE), TILE)
                stage[lax.rem(j, 4)] = lf[rows, pl.ds(half, 1024)].astype(F32)

            @pl.when(j >= 8)
            def _():
                rows = pl.ds(pl.multiple_of((j - 8) * TILE, TILE), TILE)
                stage[lax.rem(j, 4)] = bf[rows, pl.ds(half, 1024)].astype(F32)

            px(j).start()

    other = pl.multiple_of((1 - c) * 1024, 1024)

    @pl.loop(0, 12)
    def _(j):
        @pl.when(j >= last_in)
        def _():
            px(j).wait_recv()

            @pl.when(j < 8)
            def _():
                rows = pl.ds(pl.multiple_of(j * TILE, TILE), TILE)
                lf[rows, pl.ds(other, 1024)] = precv[j].astype(BF16)

            @pl.when(j >= 8)
            def _():
                rows = pl.ds(pl.multiple_of((j - 8) * TILE, TILE), TILE)
                bf[rows, pl.ds(other, 1024)] = precv[j].astype(BF16)

    for i in range(8):
        span_i = slice(i * TILE, (i + 1) * TILE)
        lf[span_i, span_i] = unit_tile(lf[span_i, span_i])
    rc(srs, srf.at[pl.ds(other, 1024)], rS, rR, partner).wait_recv()

    for d in range(1, NX):
        tx_in(d).wait_recv()
    for d in range(1, NZ):
        tz(d).start()
    for d in range(1, NZ):
        tz_in(d).wait_recv()
    cp_t = pltpu.make_async_copy(tb, ts, lsem)
    cp_t.start()
    cp_t.wait()

    xl = lax.rem(x + NX - 1, NX)
    xr = lax.rem(x + 1, NX)
    xo = lax.rem(x + 2, NX)

    def leaf_of(xx):
        return z * NX + xx

    def fwd_b(way):
        if way == 0:
            return rc(ul.at[pl.ds(0, 8)], uo.at[pl.ds(0, 8)], bS.at[0], bR.at[0], right)
        return rc(ur.at[pl.ds(8, 8)], uo.at[pl.ds(8, 8)], bS.at[1], bR.at[1], left)

    def v1_send(t, way):
        pan = pl.ds(2 * t, 2)
        dst = v1a if way == 0 else v1b
        return rc(w.at[pan], dst.at[pan], v1S.at[way, t], v1R.at[way, t], right if way == 0 else left)

    def v1_fwd(way):
        if way == 0:
            return rc(v1a.at[pl.ds(0, 4)], v1b.at[pl.ds(0, 4)], f1S.at[0], f1R.at[0], right)
        return rc(v1b.at[pl.ds(4, 4)], v1b.at[pl.ds(4, 4)], f1S.at[1], f1R.at[1], left)

    def v2_send(t, way):
        pan = pl.ds(2 * t, 2)
        return rc(w.at[pan], v2r.at[pan], v2S.at[way, t], v2R.at[t], left if way == 0 else right)

    def v2_fwd(t):
        pan = pl.ds(2 * t, 2)
        return rc(v2r.at[pan], v2r.at[pan], f2S.at[t % 2], f2R.at[t], left if t < 2 else right)

    def z_fwd(t):
        pan = pl.ds(2 * t, 2)
        return rc(v2r.at[pan], v2p.at[pan], zS.at[t], zR.at[t], at(x, lax.rem(z + 1, NZ)))

    root = at(0, 4)
    l4_owner = at(0, jnp.where(zm == 1, lax.rem(z + 1, NZ), lax.rem(z + NZ - 1, NZ)))
    root_slot = lax.rem(lax.div(z + NZ - 1, 2), 4)
    l4_slot = lax.rem(root_slot, 2)

    def v3_send(t):
        pan = pl.ds(2 * t, 2)
        return rc(w.at[pan], v3.at[l4_slot, pan], v3S.at[t], v3R.at[l4_slot, t], l4_owner)

    def v3_in(i, t):
        pan = pl.ds(2 * t, 2)
        return rc(w.at[pan], v3.at[i, pan], v3S.at[t], v3R.at[i, t], partner)

    def v5_send():
        return rc(w, v3.at[root_slot, pl.ds(0, 8)], v5S, v5R.at[root_slot], root)

    def v5_in(i):
        return rc(w, v3.at[i, pl.ds(0, 8)], v5S, v5R.at[i], partner)

    v4_slot = lax.rem(lax.div(z, 4), 2)

    def v4_send(t):
        pan = pl.ds(2 * t, 2)
        return rc(w.at[pan], v4.at[v4_slot, pan], v4S.at[t], v4R.at[v4_slot, t], root)

    def v4_in(i, t):
        pan = pl.ds(2 * t, 2)
        return rc(w.at[pan], v4.at[i, pan], v4S.at[t], v4R.at[i, t], partner)

    q_row = (
        lax.rem(z + 1, NZ),
        lax.div(z, 4) * 4 + 2,
        jnp.int32(4),
    )
    q_slot = (
        jnp.int32(0),
        jnp.where(zm == 3, 2, lax.rem(zm, 2)),
        lax.rem(jnp.where(z < 4, z, z + NZ - 1), NZ),
    )
    q_sends = (lax.rem(z, 2) == 0, zm != 2, z != 4)

    def q_send(k):
        return rc(qs.at[k], qr.at[q_slot[k]], qS.at[k], qR.at[q_slot[k]], at(x, q_row[k]))

    def q_in(i):
        return rc(qs.at[0], qr.at[i], qS.at[0], qR.at[i], partner)

    quarter = pl.ds(4 * x, 4)

    def g_send():
        return rc(qr.at[7], g.at[quarter], gS, gR.at[x], at(0, z))

    def g_in(i):
        return rc(qr.at[7], g.at[pl.ds(4 * i, 4)], gS, gR.at[i], partner)

    odd_row = jnp.where(odd, x, xl)
    odd_other = jnp.where(odd, xo, xr)

    def row_sum(lev, p):
        t = (lev - 1) * 16 + p
        acc = us[ts[l, 0, t]] + ul[ts[leaf_of(xl), 0, t]]
        acc = acc + ur[ts[leaf_of(xr), 0, t]] + uo[ts[leaf_of(xo), 0, t]]
        return acc + v1a[ts[leaf_of(odd_row), 1, t]] + v1b[ts[leaf_of(odd_other), 1, t]]

    def quarters(k, with_l2):
        @pl.loop(0, 4)
        def _(i):
            p = 4 * x + i
            acc = row_sum(k + 3, p)
            if with_l2:
                acc = acc + v2r[ts[z * NX + 2, 1, (k + 2) * 16 + p]]
            qs[k, i] = acc

    def put_res(p, value):
        rows = pl.ds(pl.multiple_of(p * PAN, PAN), PAN)
        res[rows, :] = (srf[rows, :] - value).astype(BF16)

    def collect(k, count):
        for i in range(count):
            q_in(i).wait_recv()

        @pl.loop(0, 4)
        def _(i):
            acc = qs[k, i]
            for s in range(count):
                acc = acc + qr[s, i]

            @pl.when(x == 0)
            def _():
                g[i] = acc

            @pl.when(x != 0)
            def _():
                qr[7, i] = acc

        @pl.when(x != 0)
        def _():
            g_send().start()

        @pl.when(x == 0)
        def _():
            for i in range(1, NX):
                g_in(i).wait_recv()

    width = swidth[l]

    @pl.loop(0, 5)
    def _(rnd):
        @pl.when(rnd == 0)
        def _():
            for j in range(8):
                send_a(j, 0).wait_recv()
                send_a(j, 1).wait_recv()
            fwd_b(0).start()
            fwd_b(1).start()

            @pl.when(level == 1)
            def _():
                @pl.loop(0, 16)
                def _(p):
                    put_res(p, us[ts[l, 0, p]] + ul[ts[leaf_of(xl), 0, p]])

        @pl.when(rnd == 1)
        def _():
            @pl.when(jnp.logical_not(odd))
            def _():
                for t in range(4):
                    v1_send(t, 0).wait_recv()
                    v1_send(t, 1).wait_recv()
                v1_fwd(0).start()
                v1_fwd(1).start()

            fwd_b(0).wait_recv()
            fwd_b(1).wait_recv()

            @pl.when(odd)
            def _():
                v1_fwd(0).wait_recv()
                v1_fwd(1).wait_recv()

            @pl.when(level == 2)
            def _():
                @pl.loop(0, 16)
                def _(p):
                    put_res(p, row_sum(2, p))

        @pl.when(rnd == 2)
        def _():
            quarters(0, False)

            @pl.when(q_sends[0])
            def _():
                q_send(0).start()

            @pl.when(x == 1)
            def _():
                for t in (0, 1, 2, 3):
                    v2_send(t, 0).wait_recv()
                    if t < 2:
                        v2_fwd(t).start()

            @pl.when(x == 3)
            def _():
                for t in (2, 3, 0, 1):
                    v2_send(t, 1).wait_recv()
                    if t >= 2:
                        v2_fwd(t).start()

            @pl.when(x == 0)
            def _():
                for t in (0, 2, 1, 3):
                    v2_fwd(t).wait_recv()

                    @pl.when(lax.rem(z, 2) == 0)
                    def _():
                        z_fwd(t).start()

            quarters(1, True)
            quarters(2, True)
            for k in (1, 2):
                @pl.when(q_sends[k])
                def _():
                    q_send(k).start()

            @pl.when(lax.rem(z, 2) == 1)
            def _():
                collect(0, 1)

            @pl.when(level == 3)
            def _():
                for t in range(4):
                    z_fwd(t).wait_recv()

                @pl.loop(0, 16)
                def _(p):
                    t = 2 * 16 + p
                    acc = g[p] + v2r[ts[z * NX + 2, 1, t]]
                    put_res(p, acc + v2p[ts[lax.rem(z + NZ - 1, NZ) * NX + 2, 1, t]])

        @pl.when(rnd == 3)
        def _():
            @pl.when(zm == 2)
            def _():
                collect(1, 3)

            @pl.when(z == 4)
            def _():
                collect(2, 7)

            @pl.when(level == 4)
            def _():
                for i in range(2):
                    for t in range(4):
                        v3_in(i, t).wait_recv()

                @pl.loop(0, 16)
                def _(p):
                    t = 3 * 16 + p
                    acc = g[p] + v3[0, ts[lax.rem(z + NZ - 1, NZ) * NX, 1, t]]
                    put_res(p, acc + v3[1, ts[lax.rem(z + 1, NZ) * NX, 1, t]])

        @pl.when(rnd == 4)
        def _():
            @pl.when(level == 5)
            def _():
                for i in range(4):
                    v5_in(i).wait_recv()
                for i in range(2):
                    for t in range(4):
                        v4_in(i, t).wait_recv()

                @pl.loop(0, 16)
                def _(p):
                    t = 4 * 16 + p
                    acc = g[p]
                    for i in range(4):
                        acc = acc + v3[i, ts[(2 * i + 1) * NX, 1, t]]
                    for i in range(2):
                        acc = acc + v4[i, ts[(4 * i + 2) * NX, 1, t]]
                    put_res(p, acc)

        @pl.when(level == rnd + 1)
        def _():
            for i in range(8):
                top = i * TILE
                y = mm(lf[top : top + TILE, : top + TILE], res[: top + TILE, :])
                rows = top + lax.broadcasted_iota(jnp.int32, (TILE, LANES), 0)
                yb[top : top + TILE, :] = jnp.where(rows < width, y, 0.0).astype(BF16)

            for t in (0, 2, 1, 3):
                @pl.when(level < 5)
                def _():
                    upd = mm(bf[t * TILE : (t + 1) * TILE, :], yb[...]).reshape(2, PAN, LANES)
                    w[2 * t : 2 * t + 2] = upd

                    @pl.when(level == 1)
                    def _():
                        v1a[2 * t : 2 * t + 2] = upd
                        v1_send(t, 0).start()
                        v1_send(t, 1).start()

                    @pl.when(level == 2)
                    def _():
                        v2r[2 * t : 2 * t + 2] = upd
                        v2_send(t, 0 if t < 2 else 1).start()

                    @pl.when(level == 3)
                    def _():
                        v3_send(t).start()

                    @pl.when(level == 4)
                    def _():
                        v4_send(t).start()

            @pl.when(level == 2)
            def _():
                for t in (2, 3):
                    v2_send(t, 0).start()
                for t in (0, 1):
                    v2_send(t, 1).start()

            @pl.when(level == 3)
            def _():
                v5_send().start()

    def yx():
        return rc(ysend, yrecv, yS, yR, partner)

    @pl.when(level > 0)
    def _():
        ysend[...] = yb[pl.ds(other, 1024), :].astype(F32)
        yx().start()
        mine = yb[pl.ds(half, 1024), :]
        yx().wait_recv()
        theirs = yrecv[...].astype(BF16)
        sout[:, :LANES] = jnp.where(first, mine, theirs)
        sout[:, LANES:] = jnp.where(first, theirs, mine)
        yx().wait_send()

    @pl.when(level == 0)
    def _():
        sout[...] = jnp.zeros_like(sout)

    @pl.when(c == 0)
    def _():
        for i in range(4):
            p10(i).wait_send()

    for j in range(8):
        ux(j).wait_send()
        send_a(j, 0).wait_send()
        send_a(j, 1).wait_send()
    for d in range(1, NX):
        tx(d).wait_send()
    for d in range(1, NZ):
        tz(d).wait_send()
    rx().wait_send()
    for j in range(8, 12):
        px(j).wait_send()
    fwd_b(0).wait_send()
    fwd_b(1).wait_send()

    @pl.when(odd)
    def _():
        for t in range(4):
            v1_send(t, 0).wait_send()
            v1_send(t, 1).wait_send()

    @pl.when(jnp.logical_not(odd))
    def _():
        v1_fwd(0).wait_send()
        v1_fwd(1).wait_send()

    @pl.when(x == 2)
    def _():
        for t in range(4):
            v2_send(t, 0).wait_send()
            v2_send(t, 1).wait_send()

    @pl.when(x == 1)
    def _():
        v2_fwd(0).wait_send()
        v2_fwd(1).wait_send()

    @pl.when(x == 3)
    def _():
        v2_fwd(2).wait_send()
        v2_fwd(3).wait_send()

    @pl.when(jnp.logical_and(x == 0, lax.rem(z, 2) == 0))
    def _():
        for t in range(4):
            z_fwd(t).wait_send()

    for k in range(3):
        @pl.when(q_sends[k])
        def _():
            q_send(k).wait_send()

    @pl.when(jnp.logical_and(x != 0, z != 0))
    def _():
        g_send().wait_send()

    @pl.when(level == 3)
    def _():
        for t in range(4):
            v3_send(t).wait_send()
        v5_send().wait_send()

    @pl.when(level == 4)
    def _():
        for t in range(4):
            v4_send(t).wait_send()


def on_device(
    leaf_rhs, leaf_inverse, leaf_below, leaf_rows,
    sep_rhs, sep_inverse, sep_below, sep_rows, sep_width,
):
    vmem = lambda *s, dtype=F32: pltpu.VMEM(s, dtype)
    dma = lambda *s: pltpu.SemaphoreType.DMA(s)
    pan = lambda *n: pltpu.VMEM((*n, PAN, LANES), F32)
    scratch = [
        vmem(2048, 1024, dtype=BF16),
        vmem(2048, 1024, dtype=BF16),
        vmem(1024, 256, dtype=BF16),
        vmem(1024, 256, dtype=BF16),
        vmem(2048, 2048, dtype=BF16),
        vmem(1024, 2048, dtype=BF16),
        vmem(4, 256, 1024),
        vmem(12, 256, 1024),
        pan(17), pan(17), pan(17), pan(17),
        pan(9), pan(9), pan(9), pan(9),
        pan(4, 9), pan(2, 9), pan(8),
        pan(3, 4), pan(8, 4), pan(16),
        vmem(4, 256, 256), vmem(4, 256, 256), vmem(256, 256),
        vmem(1024, 256, dtype=BF16),
        pan(8, 2), pan(8, 2),
        vmem(2048, 128), vmem(1024, 128),
        vmem(2048, 128, dtype=BF16), vmem(2048, 128, dtype=BF16),
        vmem(1024, 128), vmem(1024, 128),
        vmem(32, 8, 128, dtype=jnp.int32),
        pltpu.SMEM((32, 8, 128), jnp.int32),
        dma(7),
        dma(4), dma(4), dma(8), dma(8), dma(2, 8), dma(2, 8), dma(2), dma(2),
        dma(2, 4), dma(2, 4), dma(2), dma(2),
        dma(2, 4), dma(4), dma(2), dma(4), dma(4), dma(4),
        dma(4), dma(2, 4), pltpu.SemaphoreType.DMA, dma(4), dma(4), dma(2, 4),
        dma(3), dma(8), pltpu.SemaphoreType.DMA, dma(4), dma(12), dma(12),
        pltpu.SemaphoreType.DMA, pltpu.SemaphoreType.DMA,
        pltpu.SemaphoreType.DMA, pltpu.SemaphoreType.DMA,
        dma(3), dma(3), dma(7), dma(7), pltpu.SemaphoreType.DMA,
    ]
    smem = pl.BlockSpec(memory_space=pltpu.SMEM)
    hbm = pl.BlockSpec(memory_space=pl.ANY)
    out = pl.BlockSpec(memory_space=pltpu.VMEM)
    return pl.pallas_call(
        kernel,
        out_shape=(
            jax.ShapeDtypeStruct((1024, 256), BF16),
            jax.ShapeDtypeStruct((1024, 256), BF16),
        ),
        in_specs=[smem, smem, smem, hbm, hbm, hbm, hbm, hbm, hbm],
        out_specs=(out, out),
        scratch_shapes=scratch,
        compiler_params=pltpu.CompilerParams(
            collective_id=0, has_side_effects=True, vmem_limit_bytes=66_000_000,
        ),
        name="forward_substitution",
    )(leaf_rows, sep_rows, sep_width, leaf_rhs, leaf_inverse, leaf_below, sep_rhs, sep_inverse, sep_below)


def solution(mesh):
    placed = (
        P(("leaf", "col"), "row"),
        P("leaf", "col"),
        P("leaf", "col"),
        P("leaf", None),
        P(("leaf", "col"), "row"),
        P("leaf", "col"),
        P("leaf", "col"),
        P("leaf", None),
        P(),
    )
    return jax.shard_map(
        on_device,
        mesh=mesh,
        in_specs=placed,
        out_specs=(P(("leaf", "col"), "row"), P(("leaf", "col"), "row")),
        check_vma=False,
    )
```

```python
import jax
import jax.numpy as jnp
from jax import lax
from jax.experimental import pallas as pl
from jax.experimental.pallas import tpu as pltpu
from jax.sharding import PartitionSpec as P

MESH = pl.DeviceIdType.MESH
F32 = jnp.float32
BF16 = jnp.bfloat16
PAN = 128
TILE = 256
LANES = 128
NX = 4
NZ = 8


def mm(a, b):
    return jnp.dot(a, b, preferred_element_type=F32)


def unit_tile(block):
    rows = lax.broadcasted_iota(jnp.int32, block.shape, 0)
    cols = lax.broadcasted_iota(jnp.int32, block.shape, 1)
    kept = jnp.where(rows > cols, block.astype(F32), 0.0)
    return jnp.where(rows == cols, 1.0, kept).astype(BF16)


def kernel(
    lrows, srows, swidth, lrhs_h, linv_h, lbel_h, srhs_h, sinv_h, sbel_h,
    lout, sout,
    ll, lb, bl, sr, lf, bf, stage, precv,
    us, ul, ur, uo, v1a, v1b, v2r, v2p, v3, v4, w, qs, qr, g,
    pps, prx, dbuf, xloc, usend, urecv, srf, srs, res, yb, ysend, yrecv,
    tb, ts,
    hsem, p10s, p10r, uxs, uxr, aS, aR, bS, bR, v1S, v1R, f1S, f1R,
    v2S, v2R, f2S, f2R, zS, zR, v3S, v3R, v5S, v5R, v4S, v4R,
    qS, qR, gS, gR, pS, pR, rS, rR, yS, yR, tS, tR, tzS, tzR, lsem,
    e1S, e1R, e2S, e2R, e3S, e3R,
):
    l = lax.axis_index("leaf")
    row = lax.axis_index("row")
    c = lax.axis_index("col")
    x = lax.rem(l, NX)
    z = lax.div(l, NX)
    zm = lax.rem(z, 4)
    odd = lax.rem(x, 2) == 1
    level = jnp.where(
        odd, 1,
        jnp.where(
            x == 2, 2,
            jnp.where(
                lax.rem(z, 2) == 1, 3,
                jnp.where(zm == 2, 4, jnp.where(z == 4, 5, 0)),
            ),
        ),
    )

    def at(xx, zz):
        return (zz * NX + xx, row, c)

    right = at(lax.rem(x + 1, NX), z)
    left = at(lax.rem(x + NX - 1, NX), z)
    partner = (l, row, 1 - c)

    def rc(src, dst, ss, rs, dev):
        return pltpu.make_async_remote_copy(
            src_ref=src, dst_ref=dst, send_sem=ss, recv_sem=rs,
            device_id=dev, device_id_type=MESH,
        )

    bar = pltpu.get_barrier_semaphore()
    pl.semaphore_signal(bar, 1, device_id=partner, device_id_type=MESH)
    for d in range(1, NX):
        pl.semaphore_signal(bar, 1, device_id=at(lax.rem(x + d, NX), z), device_id_type=MESH)
    for d in range(1, NZ):
        pl.semaphore_signal(bar, 1, device_id=at(x, lax.rem(z + d, NZ)), device_id_type=MESH)

    half = pl.multiple_of(c * 1024, 1024)
    cp_rhs = pltpu.make_async_copy(lrhs_h, bl, hsem.at[0])
    cp_hi = pltpu.make_async_copy(linv_h.at[pl.ds(1024, 1024)], ll.at[pl.ds(1024, 1024)], hsem.at[1])
    cp_lo = pltpu.make_async_copy(linv_h.at[pl.ds(0, 1024)], ll.at[pl.ds(0, 1024)], hsem.at[2])
    cp_lb = pltpu.make_async_copy(lbel_h, lb, hsem.at[3])
    cp_sr = pltpu.make_async_copy(srhs_h, sr, hsem.at[4])
    cp_lf = pltpu.make_async_copy(sinv_h, lf.at[:, pl.ds(half, 1024)], hsem.at[5])
    cp_bf = pltpu.make_async_copy(sbel_h, bf.at[:, pl.ds(half, 1024)], hsem.at[6])
    for cp in (cp_rhs, cp_hi, cp_lo, cp_lb, cp_sr, cp_lf, cp_bf):
        cp.start()

    lane = lax.broadcasted_iota(jnp.int32, (8, 128), 1)
    sub = lax.broadcasted_iota(jnp.int32, (8, 128), 0)
    span = jnp.left_shift(1, lax.shift_right_logical(lane, 4) + 1)
    base = l - jnp.bitwise_and(l, span - 1) + lax.shift_right_logical(span, 1)
    target = base * 16 + jnp.bitwise_and(lane, 15)
    inv_leaf = jnp.full((8, 128), 16, jnp.int32)
    for j in range(16):
        inv_leaf = jnp.where(target == lrows[0, j], j, inv_leaf)
    inv_sep = jnp.full((8, 128), 8, jnp.int32)
    for j in range(8):
        inv_sep = jnp.where(target == srows[0, j], j, inv_sep)
    tb[l] = jnp.where(sub == 0, inv_leaf, inv_sep)

    zero_panel = jnp.zeros((PAN, LANES), F32)
    for ref in (us, ul, ur, uo):
        ref[16] = zero_panel
    for ref in (v1a, v1b, v2r, v2p):
        ref[8] = zero_panel
    for i in range(4):
        v3[i, 8] = zero_panel
    for i in range(2):
        v4[i, 8] = zero_panel

    cp_rhs.wait()
    cp_hi.wait()

    @pl.when(c == 0)
    def _():
        for i in range(4):
            pps[i] = mm(ll[1024 + i * TILE : 1024 + (i + 1) * TILE, :], bl[...])

    pl.semaphore_wait(bar, 1 + (NX - 1) + (NZ - 1))

    def p10(i):
        return rc(pps.at[i], prx.at[i], p10s.at[i], p10r.at[i], partner)

    @pl.when(c == 0)
    def _():
        for i in range(4):
            p10(i).start()

    cp_lo.wait()
    for i in range(4):
        rows = pl.ds(pl.multiple_of(c * 1024 + i * TILE, TILE), TILE)
        acc = mm(unit_tile(ll[rows, i * TILE : (i + 1) * TILE]), bl[i * TILE : (i + 1) * TILE, :])
        if i:
            acc = acc + mm(ll[rows, : i * TILE], bl[: i * TILE, :])
        dbuf[...] = acc

        @pl.when(c == 1)
        def _():
            p10(i).wait_recv()
            dbuf[...] += prx[i]

        xloc[i * TILE : (i + 1) * TILE, :] = dbuf[...].astype(BF16)
    lout[...] = xloc[...]

    cp_lb.wait()

    def ux(j):
        return rc(usend.at[j], urecv.at[j], uxs.at[j], uxr.at[j], partner)

    def send_a(j, way):
        dst = ul if way == 0 else ur
        pan = pl.ds(2 * j, 2)
        return rc(us.at[pan], dst.at[pan], aS.at[way, j], aR.at[way, j], right if way == 0 else left)

    @pl.loop(0, 9)
    def _(j):
        @pl.when(j < 8)
        def _():
            t = mm(lb[pl.ds(pl.multiple_of(j * TILE, TILE), TILE), :], xloc[...])
            lo = t[:, :LANES]
            hi = t[:, LANES:]
            first = c == 0
            us[pl.ds(2 * j, 2)] = jnp.where(first, lo, hi).reshape(2, PAN, LANES)
            usend[j] = jnp.where(first, hi, lo).reshape(2, PAN, LANES)
            ux(j).start()

        @pl.when(j > 0)
        def _():
            i = j - 1
            ux(i).wait_recv()
            us[pl.ds(2 * i, 2)] += urecv[i]
            send_a(i, 0).start()
            send_a(i, 1).start()

    def tx(d):
        return rc(tb.at[l], tb.at[l], tS.at[d - 1], tR.at[d - 1], at(lax.rem(x + d, NX), z))

    def tx_in(d):
        src = tb.at[z * NX + lax.rem(x + NX - d, NX)]
        return rc(src, src, tS.at[d - 1], tR.at[d - 1], partner)

    def tz(d):
        rows = tb.at[pl.ds(z * NX, NX)]
        return rc(rows, rows, tzS.at[d - 1], tzR.at[d - 1], at(x, lax.rem(z + d, NZ)))

    def tz_in(d):
        rows = tb.at[pl.ds(lax.rem(z + NZ - d, NZ) * NX, NX)]
        return rc(rows, rows, tzS.at[d - 1], tzR.at[d - 1], partner)

    for d in range(1, NX):
        tx(d).start()

    cp_sr.wait()
    srv = sr[...].astype(F32)
    first = c == 0
    srs[...] = jnp.where(first, srv[:, LANES:], srv[:, :LANES])

    def rx():
        return rc(srs, srf.at[pl.ds(half, 1024)], rS, rR, partner)

    rx().start()
    srf[pl.ds(half, 1024), :] = jnp.where(first, srv[:, :LANES], srv[:, LANES:])

    cp_lf.wait()
    cp_bf.wait()

    def px(j):
        return rc(stage.at[lax.rem(j, 4)], precv.at[j], pS.at[j], pR.at[j], partner)

    first_j = jnp.where(c == 0, 0, 4)
    last_in = jnp.where(c == 0, 4, 0)

    @pl.loop(0, 12)
    def _(j):
        @pl.when(j >= first_j)
        def _():
            @pl.when(j >= first_j + 4)
            def _():
                px(j - 4).wait_send()

            @pl.when(j < 8)
            def _():
                rows = pl.ds(pl.multiple_of(j * TILE, TILE), TILE)
                stage[lax.rem(j, 4)] = lf[rows, pl.ds(half, 1024)].astype(F32)

            @pl.when(j >= 8)
            def _():
                rows = pl.ds(pl.multiple_of((j - 8) * TILE, TILE), TILE)
                stage[lax.rem(j, 4)] = bf[rows, pl.ds(half, 1024)].astype(F32)

            px(j).start()

    other = pl.multiple_of((1 - c) * 1024, 1024)

    @pl.loop(0, 12)
    def _(j):
        @pl.when(j >= last_in)
        def _():
            px(j).wait_recv()

            @pl.when(j < 8)
            def _():
                rows = pl.ds(pl.multiple_of(j * TILE, TILE), TILE)
                lf[rows, pl.ds(other, 1024)] = precv[j].astype(BF16)

            @pl.when(j >= 8)
            def _():
                rows = pl.ds(pl.multiple_of((j - 8) * TILE, TILE), TILE)
                bf[rows, pl.ds(other, 1024)] = precv[j].astype(BF16)

    for i in range(8):
        span_i = slice(i * TILE, (i + 1) * TILE)
        lf[span_i, span_i] = unit_tile(lf[span_i, span_i])
    rc(srs, srf.at[pl.ds(other, 1024)], rS, rR, partner).wait_recv()

    for d in range(1, NX):
        tx_in(d).wait_recv()
    for d in range(1, NZ):
        tz(d).start()
    for d in range(1, NZ):
        tz_in(d).wait_recv()
    cp_t = pltpu.make_async_copy(tb, ts, lsem)
    cp_t.start()
    cp_t.wait()

    xl = lax.rem(x + NX - 1, NX)
    xr = lax.rem(x + 1, NX)
    xo = lax.rem(x + 2, NX)

    def leaf_of(xx):
        return z * NX + xx

    def fwd_b(way):
        if way == 0:
            return rc(ul.at[pl.ds(0, 8)], uo.at[pl.ds(0, 8)], bS.at[0], bR.at[0], right)
        return rc(ur.at[pl.ds(8, 8)], uo.at[pl.ds(8, 8)], bS.at[1], bR.at[1], left)

    def v1_send(t, way):
        pan = pl.ds(2 * t, 2)
        dst = v1a if way == 0 else v1b
        return rc(w.at[pan], dst.at[pan], v1S.at[way, t], v1R.at[way, t], right if way == 0 else left)

    def v1_fwd(way):
        if way == 0:
            return rc(v1a.at[pl.ds(0, 4)], v1b.at[pl.ds(0, 4)], f1S.at[0], f1R.at[0], right)
        return rc(v1b.at[pl.ds(4, 4)], v1b.at[pl.ds(4, 4)], f1S.at[1], f1R.at[1], left)

    def v2_send(t, way):
        pan = pl.ds(2 * t, 2)
        return rc(w.at[pan], v2r.at[pan], v2S.at[way, t], v2R.at[t], left if way == 0 else right)

    def v2_fwd(t):
        pan = pl.ds(2 * t, 2)
        return rc(v2r.at[pan], v2r.at[pan], f2S.at[t % 2], f2R.at[t], left if t < 2 else right)

    def z_fwd(t):
        pan = pl.ds(2 * t, 2)
        return rc(v2r.at[pan], v2p.at[pan], zS.at[t], zR.at[t], at(x, lax.rem(z + 1, NZ)))

    root = at(0, 4)
    l4_owner = at(0, jnp.where(zm == 1, lax.rem(z + 1, NZ), lax.rem(z + NZ - 1, NZ)))
    root_slot = lax.rem(lax.div(z + NZ - 1, 2), 4)
    l4_slot = lax.rem(root_slot, 2)

    def v3_send(t):
        pan = pl.ds(2 * t, 2)
        return rc(w.at[pan], v3.at[l4_slot, pan], v3S.at[t], v3R.at[l4_slot, t], l4_owner)

    def v3_in(i, t):
        pan = pl.ds(2 * t, 2)
        return rc(w.at[pan], v3.at[i, pan], v3S.at[t], v3R.at[i, t], partner)

    def v5_send():
        return rc(w, v3.at[root_slot, pl.ds(0, 8)], v5S, v5R.at[root_slot], root)

    def v5_in(i):
        return rc(w, v3.at[i, pl.ds(0, 8)], v5S, v5R.at[i], partner)

    far = jnp.logical_or(z == 1, z == 7)
    side = jnp.where(z < 4, 1, 3)
    far_slot = jnp.where(z == 4, jnp.where(x == 1, 0, 3), root_slot)
    first_relay = jnp.logical_and(far, x == side)
    last_relay = jnp.logical_and(z == 4, odd)

    def e1(t, dev):
        pan = pl.ds(2 * t, 2)
        return rc(w.at[pan], v3.at[far_slot, pan], e1S.at[t], e1R.at[t], dev)

    def e2(t, dev):
        pan = pl.ds(2 * t, 2)
        return rc(v3.at[far_slot, pan], v3.at[far_slot, pan], e2S.at[t], e2R.at[t], dev)

    def e3(t):
        pan = pl.ds(2 * t, 2)
        half_i = jnp.where(x == 1, 0, 1)
        return rc(v3.at[far_slot, pan], v3.at[far_slot, pan], e3S.at[t], e3R.at[half_i, t], root)

    def e3_in(i, t):
        pan = pl.ds(2 * t, 2)
        return rc(w.at[pan], v3.at[3 * i, pan], e3S.at[t], e3R.at[i, t], partner)

    v4_slot = lax.rem(lax.div(z, 4), 2)

    def v4_send(t):
        pan = pl.ds(2 * t, 2)
        return rc(w.at[pan], v4.at[v4_slot, pan], v4S.at[t], v4R.at[v4_slot, t], root)

    def v4_in(i, t):
        pan = pl.ds(2 * t, 2)
        return rc(w.at[pan], v4.at[i, pan], v4S.at[t], v4R.at[i, t], partner)

    q_row = (
        lax.rem(z + 1, NZ),
        lax.div(z, 4) * 4 + 2,
        jnp.int32(4),
    )
    q_slot = (
        jnp.int32(0),
        jnp.where(zm == 3, 2, lax.rem(zm, 2)),
        lax.rem(jnp.where(z < 4, z, z + NZ - 1), NZ),
    )
    q_sends = (lax.rem(z, 2) == 0, zm != 2, z != 4)

    def q_send(k):
        return rc(qs.at[k], qr.at[q_slot[k]], qS.at[k], qR.at[q_slot[k]], at(x, q_row[k]))

    def q_in(i):
        return rc(qs.at[0], qr.at[i], qS.at[0], qR.at[i], partner)

    quarter = pl.ds(4 * x, 4)

    def g_send():
        return rc(qr.at[7], g.at[quarter], gS, gR.at[x], at(0, z))

    def g_in(i):
        return rc(qr.at[7], g.at[pl.ds(4 * i, 4)], gS, gR.at[i], partner)

    odd_row = jnp.where(odd, x, xl)
    odd_other = jnp.where(odd, xo, xr)

    def row_sum(lev, p):
        t = (lev - 1) * 16 + p
        acc = us[ts[l, 0, t]] + ul[ts[leaf_of(xl), 0, t]]
        acc = acc + ur[ts[leaf_of(xr), 0, t]] + uo[ts[leaf_of(xo), 0, t]]
        return acc + v1a[ts[leaf_of(odd_row), 1, t]] + v1b[ts[leaf_of(odd_other), 1, t]]

    def quarters(k, with_l2):
        @pl.loop(0, 4)
        def _(i):
            p = 4 * x + i
            acc = row_sum(k + 3, p)
            if with_l2:
                acc = acc + v2r[ts[z * NX + 2, 1, (k + 2) * 16 + p]]
            qs[k, i] = acc

    def put_res(p, value):
        rows = pl.ds(pl.multiple_of(p * PAN, PAN), PAN)
        res[rows, :] = (srf[rows, :] - value).astype(BF16)

    def collect(k, count, main):
        for i in range(count):
            q_in(i).wait_recv()

        @pl.loop(0, 4)
        def _(i):
            acc = qs[k, i]
            for s in range(count):
                acc = acc + qr[s, i]
            if main:
                g[i] = acc
            else:
                qr[7, i] = acc

        if main:
            for i in range(1, NX):
                g_in(i).wait_recv()
        else:
            g_send().start()

    width = swidth[l]

    @pl.loop(0, 5)
    def _(rnd):
        @pl.when(rnd == 0)
        def _():
            for j in range(8):
                send_a(j, 0).wait_recv()
                send_a(j, 1).wait_recv()
            fwd_b(0).start()
            fwd_b(1).start()

            @pl.when(level == 1)
            def _():
                @pl.loop(0, 16)
                def _(p):
                    put_res(p, us[ts[l, 0, p]] + ul[ts[leaf_of(xl), 0, p]])

        @pl.when(rnd == 1)
        def _():
            @pl.when(jnp.logical_not(odd))
            def _():
                for t in range(4):
                    v1_send(t, 0).wait_recv()
                    v1_send(t, 1).wait_recv()
                v1_fwd(0).start()
                v1_fwd(1).start()

            fwd_b(0).wait_recv()
            fwd_b(1).wait_recv()

            @pl.when(odd)
            def _():
                v1_fwd(0).wait_recv()
                v1_fwd(1).wait_recv()

            quarters(0, False)

            @pl.when(q_sends[0])
            def _():
                q_send(0).start()

            @pl.when(level == 2)
            def _():
                @pl.loop(0, 16)
                def _(p):
                    put_res(p, row_sum(2, p))

        @pl.when(rnd == 2)
        def _():
            @pl.when(jnp.logical_and(lax.rem(z, 2) == 1, x != 0))
            def _():
                collect(0, 1, False)

            @pl.when(x == 1)
            def _():
                for t in (0, 1, 2, 3):
                    v2_send(t, 0).wait_recv()
                    if t < 2:
                        v2_fwd(t).start()

            @pl.when(x == 3)
            def _():
                for t in (2, 3, 0, 1):
                    v2_send(t, 1).wait_recv()
                    if t >= 2:
                        v2_fwd(t).start()

            @pl.when(x == 0)
            def _():
                for t in (0, 2, 1, 3):
                    v2_fwd(t).wait_recv()

                    @pl.when(lax.rem(z, 2) == 0)
                    def _():
                        z_fwd(t).start()

            quarters(1, True)
            quarters(2, True)
            for k in (1, 2):
                @pl.when(q_sends[k])
                def _():
                    q_send(k).start()

            @pl.when(level == 3)
            def _():
                collect(0, 1, True)

            @pl.when(level == 3)
            def _():
                for t in range(4):
                    z_fwd(t).wait_recv()

                @pl.loop(0, 16)
                def _(p):
                    t = 2 * 16 + p
                    acc = g[p] + v2r[ts[z * NX + 2, 1, t]]
                    put_res(p, acc + v2p[ts[lax.rem(z + NZ - 1, NZ) * NX + 2, 1, t]])

        @pl.when(rnd == 3)
        def _():
            @pl.when(jnp.logical_and(zm == 2, x == 0))
            def _():
                collect(1, 3, True)

            @pl.when(jnp.logical_and(zm == 2, x != 0))
            def _():
                collect(1, 3, False)

            @pl.when(jnp.logical_and(z == 4, x == 0))
            def _():
                collect(2, 7, True)

            @pl.when(jnp.logical_and(z == 4, x != 0))
            def _():
                collect(2, 7, False)

            @pl.when(level == 4)
            def _():
                for i in range(2):
                    for t in range(4):
                        v3_in(i, t).wait_recv()

                @pl.loop(0, 16)
                def _(p):
                    t = 3 * 16 + p
                    acc = g[p] + v3[0, ts[lax.rem(z + NZ - 1, NZ) * NX, 1, t]]
                    put_res(p, acc + v3[1, ts[lax.rem(z + 1, NZ) * NX, 1, t]])

        @pl.when(rnd == 4)
        def _():
            @pl.when(first_relay)
            def _():
                for t in (0, 2, 1, 3):
                    e1(t, partner).wait_recv()
                    e2(t, at(x, 4)).start()

            @pl.when(last_relay)
            def _():
                for t in (0, 2, 1, 3):
                    e2(t, partner).wait_recv()
                    e3(t).start()

            @pl.when(level == 5)
            def _():
                for i in (1, 2):
                    v5_in(i).wait_recv()
                for i in range(2):
                    for t in range(4):
                        e3_in(i, t).wait_recv()
                for i in range(2):
                    for t in range(4):
                        v4_in(i, t).wait_recv()

                @pl.loop(0, 16)
                def _(p):
                    t = 4 * 16 + p
                    acc = g[p]
                    for i in range(4):
                        acc = acc + v3[i, ts[(2 * i + 1) * NX, 1, t]]
                    for i in range(2):
                        acc = acc + v4[i, ts[(4 * i + 2) * NX, 1, t]]
                    put_res(p, acc)

        @pl.when(level == rnd + 1)
        def _():
            for i in range(8):
                top = i * TILE
                y = mm(lf[top : top + TILE, : top + TILE], res[: top + TILE, :])
                rows = top + lax.broadcasted_iota(jnp.int32, (TILE, LANES), 0)
                yb[top : top + TILE, :] = jnp.where(rows < width, y, 0.0).astype(BF16)

            for t in (0, 2, 1, 3):
                @pl.when(level < 5)
                def _():
                    upd = mm(bf[t * TILE : (t + 1) * TILE, :], yb[...]).reshape(2, PAN, LANES)
                    w[2 * t : 2 * t + 2] = upd

                    @pl.when(level == 1)
                    def _():
                        v1a[2 * t : 2 * t + 2] = upd
                        v1_send(t, 0).start()
                        v1_send(t, 1).start()

                    @pl.when(level == 2)
                    def _():
                        v2r[2 * t : 2 * t + 2] = upd
                        v2_send(t, 0 if t < 2 else 1).start()

                    @pl.when(level == 3)
                    def _():
                        v3_send(t).start()

                    @pl.when(level == 4)
                    def _():
                        v4_send(t).start()

            @pl.when(level == 2)
            def _():
                for t in (2, 3):
                    v2_send(t, 0).start()
                for t in (0, 1):
                    v2_send(t, 1).start()

            @pl.when(jnp.logical_and(level == 3, far))
            def _():
                for t in (0, 2, 1, 3):
                    e1(t, at(side, z)).start()

            @pl.when(jnp.logical_and(level == 3, jnp.logical_not(far)))
            def _():
                v5_send().start()

    def yx():
        return rc(ysend, yrecv, yS, yR, partner)

    @pl.when(level > 0)
    def _():
        ysend[...] = yb[pl.ds(other, 1024), :].astype(F32)
        yx().start()
        mine = yb[pl.ds(half, 1024), :]
        yx().wait_recv()
        theirs = yrecv[...].astype(BF16)
        sout[:, :LANES] = jnp.where(first, mine, theirs)
        sout[:, LANES:] = jnp.where(first, theirs, mine)
        yx().wait_send()

    @pl.when(level == 0)
    def _():
        sout[...] = jnp.zeros_like(sout)

    @pl.when(c == 0)
    def _():
        for i in range(4):
            p10(i).wait_send()

    for j in range(8):
        ux(j).wait_send()
        send_a(j, 0).wait_send()
        send_a(j, 1).wait_send()
    for d in range(1, NX):
        tx(d).wait_send()
    for d in range(1, NZ):
        tz(d).wait_send()
    rx().wait_send()
    for j in range(8, 12):
        px(j).wait_send()
    fwd_b(0).wait_send()
    fwd_b(1).wait_send()

    @pl.when(odd)
    def _():
        for t in range(4):
            v1_send(t, 0).wait_send()
            v1_send(t, 1).wait_send()

    @pl.when(jnp.logical_not(odd))
    def _():
        v1_fwd(0).wait_send()
        v1_fwd(1).wait_send()

    @pl.when(x == 2)
    def _():
        for t in range(4):
            v2_send(t, 0).wait_send()
            v2_send(t, 1).wait_send()

    @pl.when(x == 1)
    def _():
        v2_fwd(0).wait_send()
        v2_fwd(1).wait_send()

    @pl.when(x == 3)
    def _():
        v2_fwd(2).wait_send()
        v2_fwd(3).wait_send()

    @pl.when(jnp.logical_and(x == 0, lax.rem(z, 2) == 0))
    def _():
        for t in range(4):
            z_fwd(t).wait_send()

    for k in range(3):
        @pl.when(q_sends[k])
        def _():
            q_send(k).wait_send()

    @pl.when(jnp.logical_and(x != 0, z != 0))
    def _():
        g_send().wait_send()

    @pl.when(level == 3)
    def _():
        for t in range(4):
            v3_send(t).wait_send()

    @pl.when(jnp.logical_and(level == 3, far))
    def _():
        for t in range(4):
            e1(t, at(side, z)).wait_send()

    @pl.when(jnp.logical_and(level == 3, jnp.logical_not(far)))
    def _():
        v5_send().wait_send()

    @pl.when(first_relay)
    def _():
        for t in range(4):
            e2(t, at(x, 4)).wait_send()

    @pl.when(last_relay)
    def _():
        for t in range(4):
            e3(t).wait_send()

    @pl.when(level == 4)
    def _():
        for t in range(4):
            v4_send(t).wait_send()


def on_device(
    leaf_rhs, leaf_inverse, leaf_below, leaf_rows,
    sep_rhs, sep_inverse, sep_below, sep_rows, sep_width,
):
    vmem = lambda *s, dtype=F32: pltpu.VMEM(s, dtype)
    dma = lambda *s: pltpu.SemaphoreType.DMA(s)
    pan = lambda *n: pltpu.VMEM((*n, PAN, LANES), F32)
    scratch = [
        vmem(2048, 1024, dtype=BF16),
        vmem(2048, 1024, dtype=BF16),
        vmem(1024, 256, dtype=BF16),
        vmem(1024, 256, dtype=BF16),
        vmem(2048, 2048, dtype=BF16),
        vmem(1024, 2048, dtype=BF16),
        vmem(4, 256, 1024),
        vmem(12, 256, 1024),
        pan(17), pan(17), pan(17), pan(17),
        pan(9), pan(9), pan(9), pan(9),
        pan(4, 9), pan(2, 9), pan(8),
        pan(3, 4), pan(8, 4), pan(16),
        vmem(4, 256, 256), vmem(4, 256, 256), vmem(256, 256),
        vmem(1024, 256, dtype=BF16),
        pan(8, 2), pan(8, 2),
        vmem(2048, 128), vmem(1024, 128),
        vmem(2048, 128, dtype=BF16), vmem(2048, 128, dtype=BF16),
        vmem(1024, 128), vmem(1024, 128),
        vmem(32, 8, 128, dtype=jnp.int32),
        pltpu.SMEM((32, 8, 128), jnp.int32),
        dma(7),
        dma(4), dma(4), dma(8), dma(8), dma(2, 8), dma(2, 8), dma(2), dma(2),
        dma(2, 4), dma(2, 4), dma(2), dma(2),
        dma(2, 4), dma(4), dma(2), dma(4), dma(4), dma(4),
        dma(4), dma(2, 4), pltpu.SemaphoreType.DMA, dma(4), dma(4), dma(2, 4),
        dma(3), dma(8), pltpu.SemaphoreType.DMA, dma(4), dma(12), dma(12),
        pltpu.SemaphoreType.DMA, pltpu.SemaphoreType.DMA,
        pltpu.SemaphoreType.DMA, pltpu.SemaphoreType.DMA,
        dma(3), dma(3), dma(7), dma(7), pltpu.SemaphoreType.DMA,
        dma(4), dma(4), dma(4), dma(4), dma(4), dma(2, 4),
    ]
    smem = pl.BlockSpec(memory_space=pltpu.SMEM)
    hbm = pl.BlockSpec(memory_space=pl.ANY)
    out = pl.BlockSpec(memory_space=pltpu.VMEM)
    return pl.pallas_call(
        kernel,
        out_shape=(
            jax.ShapeDtypeStruct((1024, 256), BF16),
            jax.ShapeDtypeStruct((1024, 256), BF16),
        ),
        in_specs=[smem, smem, smem, hbm, hbm, hbm, hbm, hbm, hbm],
        out_specs=(out, out),
        scratch_shapes=scratch,
        compiler_params=pltpu.CompilerParams(
            collective_id=0, has_side_effects=True, vmem_limit_bytes=66_000_000,
        ),
        name="forward_substitution",
    )(leaf_rows, sep_rows, sep_width, leaf_rhs, leaf_inverse, leaf_below, sep_rhs, sep_inverse, sep_below)


def solution(mesh):
    placed = (
        P(("leaf", "col"), "row"),
        P("leaf", "col"),
        P("leaf", "col"),
        P("leaf", None),
        P(("leaf", "col"), "row"),
        P("leaf", "col"),
        P("leaf", "col"),
        P("leaf", None),
        P(),
    )
    return jax.shard_map(
        on_device,
        mesh=mesh,
        in_specs=placed,
        out_specs=(P(("leaf", "col"), "row"), P(("leaf", "col"), "row")),
        check_vma=False,
    )
```

```python
import jax
import jax.numpy as jnp
from jax import lax
from jax.experimental import pallas as pl
from jax.experimental.pallas import tpu as pltpu
from jax.sharding import PartitionSpec as P

MESH = pl.DeviceIdType.MESH
F32 = jnp.float32
BF16 = jnp.bfloat16
PAN = 128
TILE = 256
LANES = 128
NX = 4
NZ = 8


def mm(a, b):
    return jnp.dot(a, b, preferred_element_type=F32)


def unit_tile(block):
    rows = lax.broadcasted_iota(jnp.int32, block.shape, 0)
    cols = lax.broadcasted_iota(jnp.int32, block.shape, 1)
    kept = jnp.where(rows > cols, block.astype(F32), 0.0)
    return jnp.where(rows == cols, 1.0, kept).astype(BF16)


def kernel(
    lrows, srows, swidth, lrhs_h, linv_h, lbel_h, srhs_h, sinv_h, sbel_h,
    lout, sout,
    ll, lb, bl, sr, lf, bf, stage, precv,
    us, ul, ur, uo, v1a, v1b, v2r, v2p, v3, v4, w, qs, qr, g,
    pps, prx, dbuf, xloc, usend, urecv, srf, srs, res, yb, ysend, yrecv,
    tb, ts,
    hsem, p10s, p10r, uxs, uxr, aS, aR, bS, bR, v1S, v1R, f1S, f1R,
    v2S, v2R, f2S, f2R, zS, zR, v3S, v3R, v5S, v5R, v4S, v4R,
    qS, qR, gS, gR, pS, pR, rS, rR, yS, yR, tS, tR, tzS, tzR, lsem,
    e1S, e1R, e2S, e2R, e3S, e3R,
):
    l = lax.axis_index("leaf")
    row = lax.axis_index("row")
    c = lax.axis_index("col")
    x = lax.rem(l, NX)
    z = lax.div(l, NX)
    zm = lax.rem(z, 4)
    odd = lax.rem(x, 2) == 1
    level = jnp.where(
        odd, 1,
        jnp.where(
            x == 2, 2,
            jnp.where(
                lax.rem(z, 2) == 1, 3,
                jnp.where(zm == 2, 4, jnp.where(z == 4, 5, 0)),
            ),
        ),
    )

    def at(xx, zz):
        return (zz * NX + xx, row, c)

    right = at(lax.rem(x + 1, NX), z)
    left = at(lax.rem(x + NX - 1, NX), z)
    partner = (l, row, 1 - c)

    def rc(src, dst, ss, rs, dev):
        return pltpu.make_async_remote_copy(
            src_ref=src, dst_ref=dst, send_sem=ss, recv_sem=rs,
            device_id=dev, device_id_type=MESH,
        )

    bar = pltpu.get_barrier_semaphore()
    pl.semaphore_signal(bar, 1, device_id=partner, device_id_type=MESH)
    for d in range(1, NX):
        pl.semaphore_signal(bar, 1, device_id=at(lax.rem(x + d, NX), z), device_id_type=MESH)
    for d in range(1, NZ):
        pl.semaphore_signal(bar, 1, device_id=at(x, lax.rem(z + d, NZ)), device_id_type=MESH)

    half = pl.multiple_of(c * 1024, 1024)
    cp_rhs = pltpu.make_async_copy(lrhs_h, bl, hsem.at[0])
    cp_hi = pltpu.make_async_copy(linv_h.at[pl.ds(1024, 1024)], ll.at[pl.ds(1024, 1024)], hsem.at[1])
    cp_lo = pltpu.make_async_copy(linv_h.at[pl.ds(0, 1024)], ll.at[pl.ds(0, 1024)], hsem.at[2])
    cp_lb = pltpu.make_async_copy(lbel_h, lb, hsem.at[3])
    cp_sr = pltpu.make_async_copy(srhs_h, sr, hsem.at[4])
    cp_lf = pltpu.make_async_copy(sinv_h, lf.at[:, pl.ds(half, 1024)], hsem.at[5])
    cp_bf = pltpu.make_async_copy(sbel_h, bf.at[:, pl.ds(half, 1024)], hsem.at[6])
    for cp in (cp_rhs, cp_hi, cp_lo, cp_lb, cp_sr, cp_lf, cp_bf):
        cp.start()

    lane = lax.broadcasted_iota(jnp.int32, (8, 128), 1)
    sub = lax.broadcasted_iota(jnp.int32, (8, 128), 0)
    span = jnp.left_shift(1, lax.shift_right_logical(lane, 4) + 1)
    base = l - jnp.bitwise_and(l, span - 1) + lax.shift_right_logical(span, 1)
    target = base * 16 + jnp.bitwise_and(lane, 15)
    inv_leaf = jnp.full((8, 128), 16, jnp.int32)
    for j in range(16):
        inv_leaf = jnp.where(target == lrows[0, j], j, inv_leaf)
    inv_sep = jnp.full((8, 128), 8, jnp.int32)
    for j in range(8):
        inv_sep = jnp.where(target == srows[0, j], j, inv_sep)
    tb[l] = jnp.where(sub == 0, inv_leaf, inv_sep)

    zero_panel = jnp.zeros((PAN, LANES), F32)
    for ref in (us, ul, ur, uo):
        ref[16] = zero_panel
    for ref in (v1a, v1b, v2r, v2p):
        ref[8] = zero_panel
    for i in range(4):
        v3[i, 8] = zero_panel
    for i in range(2):
        v4[i, 8] = zero_panel

    cp_rhs.wait()
    cp_hi.wait()

    @pl.when(c == 0)
    def _():
        for i in range(4):
            pps[i] = mm(ll[1024 + i * TILE : 1024 + (i + 1) * TILE, :], bl[...])

    pl.semaphore_wait(bar, 1 + (NX - 1) + (NZ - 1))

    def p10(i):
        return rc(pps.at[i], prx.at[i], p10s.at[i], p10r.at[i], partner)

    @pl.when(c == 0)
    def _():
        for i in range(4):
            p10(i).start()

    cp_lo.wait()
    for i in range(4):
        rows = pl.ds(pl.multiple_of(c * 1024 + i * TILE, TILE), TILE)
        acc = mm(unit_tile(ll[rows, i * TILE : (i + 1) * TILE]), bl[i * TILE : (i + 1) * TILE, :])
        if i:
            acc = acc + mm(ll[rows, : i * TILE], bl[: i * TILE, :])
        dbuf[...] = acc

        @pl.when(c == 1)
        def _():
            p10(i).wait_recv()
            dbuf[...] += prx[i]

        xloc[i * TILE : (i + 1) * TILE, :] = dbuf[...].astype(BF16)
    lout[...] = xloc[...]

    cp_lb.wait()

    def ux(j):
        return rc(usend.at[j], urecv.at[j], uxs.at[j], uxr.at[j], partner)

    def send_a(j, way):
        dst = ul if way == 0 else ur
        pan = pl.ds(2 * j, 2)
        return rc(us.at[pan], dst.at[pan], aS.at[way, j], aR.at[way, j], right if way == 0 else left)

    @pl.loop(0, 9)
    def _(j):
        @pl.when(j < 8)
        def _():
            t = mm(lb[pl.ds(pl.multiple_of(j * TILE, TILE), TILE), :], xloc[...])
            lo = t[:, :LANES]
            hi = t[:, LANES:]
            first = c == 0
            us[pl.ds(2 * j, 2)] = jnp.where(first, lo, hi).reshape(2, PAN, LANES)
            usend[j] = jnp.where(first, hi, lo).reshape(2, PAN, LANES)
            ux(j).start()

        @pl.when(j > 0)
        def _():
            i = j - 1
            ux(i).wait_recv()
            us[pl.ds(2 * i, 2)] += urecv[i]
            send_a(i, 0).start()
            send_a(i, 1).start()

    def tx(d):
        return rc(tb.at[l], tb.at[l], tS.at[d - 1], tR.at[d - 1], at(lax.rem(x + d, NX), z))

    def tx_in(d):
        src = tb.at[z * NX + lax.rem(x + NX - d, NX)]
        return rc(src, src, tS.at[d - 1], tR.at[d - 1], partner)

    def tz(d):
        rows = tb.at[pl.ds(z * NX, NX)]
        return rc(rows, rows, tzS.at[d - 1], tzR.at[d - 1], at(x, lax.rem(z + d, NZ)))

    def tz_in(d):
        rows = tb.at[pl.ds(lax.rem(z + NZ - d, NZ) * NX, NX)]
        return rc(rows, rows, tzS.at[d - 1], tzR.at[d - 1], partner)

    for d in range(1, NX):
        tx(d).start()

    cp_sr.wait()
    srv = sr[...].astype(F32)
    first = c == 0
    srs[...] = jnp.where(first, srv[:, LANES:], srv[:, :LANES])

    def rx():
        return rc(srs, srf.at[pl.ds(half, 1024)], rS, rR, partner)

    rx().start()
    srf[pl.ds(half, 1024), :] = jnp.where(first, srv[:, :LANES], srv[:, LANES:])

    cp_lf.wait()
    cp_bf.wait()

    def px(j):
        return rc(stage.at[lax.rem(j, 4)], precv.at[j], pS.at[j], pR.at[j], partner)

    first_j = jnp.where(c == 0, 0, 4)
    last_in = jnp.where(c == 0, 4, 0)

    @pl.loop(0, 12)
    def _(j):
        @pl.when(j >= first_j)
        def _():
            @pl.when(j >= first_j + 4)
            def _():
                px(j - 4).wait_send()

            @pl.when(j < 8)
            def _():
                rows = pl.ds(pl.multiple_of(j * TILE, TILE), TILE)
                stage[lax.rem(j, 4)] = lf[rows, pl.ds(half, 1024)].astype(F32)

            @pl.when(j >= 8)
            def _():
                rows = pl.ds(pl.multiple_of((j - 8) * TILE, TILE), TILE)
                stage[lax.rem(j, 4)] = bf[rows, pl.ds(half, 1024)].astype(F32)

            px(j).start()

    other = pl.multiple_of((1 - c) * 1024, 1024)

    @pl.loop(0, 12)
    def _(j):
        @pl.when(j >= last_in)
        def _():
            px(j).wait_recv()

            @pl.when(j < 8)
            def _():
                rows = pl.ds(pl.multiple_of(j * TILE, TILE), TILE)
                lf[rows, pl.ds(other, 1024)] = precv[j].astype(BF16)

            @pl.when(j >= 8)
            def _():
                rows = pl.ds(pl.multiple_of((j - 8) * TILE, TILE), TILE)
                bf[rows, pl.ds(other, 1024)] = precv[j].astype(BF16)

    for i in range(8):
        span_i = slice(i * TILE, (i + 1) * TILE)
        lf[span_i, span_i] = unit_tile(lf[span_i, span_i])
    rc(srs, srf.at[pl.ds(other, 1024)], rS, rR, partner).wait_recv()

    for d in range(1, NX):
        tx_in(d).wait_recv()
    for d in range(1, NZ):
        tz(d).start()
    for d in range(1, NZ):
        tz_in(d).wait_recv()
    cp_t = pltpu.make_async_copy(tb, ts, lsem)
    cp_t.start()
    cp_t.wait()

    xl = lax.rem(x + NX - 1, NX)
    xr = lax.rem(x + 1, NX)
    xo = lax.rem(x + 2, NX)

    def leaf_of(xx):
        return z * NX + xx

    def fwd_b(way):
        if way == 0:
            return rc(ul.at[pl.ds(0, 8)], uo.at[pl.ds(0, 8)], bS.at[0], bR.at[0], right)
        return rc(ur.at[pl.ds(8, 8)], uo.at[pl.ds(8, 8)], bS.at[1], bR.at[1], left)

    def v1_send(t, way):
        pan = pl.ds(2 * t, 2)
        dst = v1a if way == 0 else v1b
        return rc(w.at[pan], dst.at[pan], v1S.at[way, t], v1R.at[way, t], right if way == 0 else left)

    def v1_fwd(way):
        if way == 0:
            return rc(v1a.at[pl.ds(0, 4)], v1b.at[pl.ds(0, 4)], f1S.at[0], f1R.at[0], right)
        return rc(v1b.at[pl.ds(4, 4)], v1b.at[pl.ds(4, 4)], f1S.at[1], f1R.at[1], left)

    def v2_send(t, way):
        pan = pl.ds(2 * t, 2)
        return rc(w.at[pan], v2r.at[pan], v2S.at[way, t], v2R.at[t], left if way == 0 else right)

    def v2_fwd(t):
        pan = pl.ds(2 * t, 2)
        return rc(v2r.at[pan], v2r.at[pan], f2S.at[t % 2], f2R.at[t], left if t < 2 else right)

    def z_fwd(t):
        pan = pl.ds(2 * t, 2)
        return rc(v2r.at[pan], v2p.at[pan], zS.at[t], zR.at[t], at(x, lax.rem(z + 1, NZ)))

    root = at(0, 4)
    l4_owner = at(0, jnp.where(zm == 1, lax.rem(z + 1, NZ), lax.rem(z + NZ - 1, NZ)))
    root_slot = lax.rem(lax.div(z + NZ - 1, 2), 4)
    l4_slot = lax.rem(root_slot, 2)

    def v3_send(t):
        pan = pl.ds(2 * t, 2)
        return rc(w.at[pan], v3.at[l4_slot, pan], v3S.at[t], v3R.at[l4_slot, t], l4_owner)

    def v3_in(i, t):
        pan = pl.ds(2 * t, 2)
        return rc(w.at[pan], v3.at[i, pan], v3S.at[t], v3R.at[i, t], partner)

    def v5_send():
        return rc(w, v3.at[root_slot, pl.ds(0, 8)], v5S, v5R.at[root_slot], root)

    def v5_in(i):
        return rc(w, v3.at[i, pl.ds(0, 8)], v5S, v5R.at[i], partner)

    far = jnp.logical_or(z == 1, z == 7)
    side = jnp.where(z < 4, 1, 3)
    far_slot = jnp.where(z == 4, jnp.where(x == 1, 0, 3), root_slot)
    first_relay = jnp.logical_and(far, x == side)
    last_relay = jnp.logical_and(z == 4, odd)

    def e1(t, dev):
        pan = pl.ds(2 * t, 2)
        return rc(w.at[pan], v3.at[far_slot, pan], e1S.at[t], e1R.at[t], dev)

    def e2(t, dev):
        pan = pl.ds(2 * t, 2)
        return rc(v3.at[far_slot, pan], v3.at[far_slot, pan], e2S.at[t], e2R.at[t], dev)

    def e3(t):
        pan = pl.ds(2 * t, 2)
        half_i = jnp.where(x == 1, 0, 1)
        return rc(v3.at[far_slot, pan], v3.at[far_slot, pan], e3S.at[t], e3R.at[half_i, t], root)

    def e3_in(i, t):
        pan = pl.ds(2 * t, 2)
        return rc(w.at[pan], v3.at[3 * i, pan], e3S.at[t], e3R.at[i, t], partner)

    v4_slot = lax.rem(lax.div(z, 4), 2)

    def v4_send(t):
        pan = pl.ds(2 * t, 2)
        return rc(w.at[pan], v4.at[v4_slot, pan], v4S.at[t], v4R.at[v4_slot, t], root)

    def v4_in(i, t):
        pan = pl.ds(2 * t, 2)
        return rc(w.at[pan], v4.at[i, pan], v4S.at[t], v4R.at[i, t], partner)

    q_row = (
        lax.rem(z + 1, NZ),
        lax.div(z, 4) * 4 + 2,
        jnp.where(z == 0, 1, 4),
    )
    q_slot = (
        jnp.int32(0),
        jnp.where(zm == 3, 2, lax.rem(zm, 2)),
        jnp.where(z == 0, 1, jnp.where(z < 4, z + NZ - 1, z + NZ - 2) - NZ),
    )
    q_sends = (lax.rem(z, 2) == 0, zm != 2, z != 4)

    def q_send(k):
        return rc(qs.at[k], qr.at[q_slot[k]], qS.at[k], qR.at[q_slot[k]], at(x, q_row[k]))

    def q_in(i):
        return rc(qs.at[0], qr.at[i], qS.at[0], qR.at[i], partner)

    quarter = pl.ds(4 * x, 4)

    def g_send():
        return rc(qr.at[7], g.at[quarter], gS, gR.at[x], at(0, z))

    def g_in(i):
        return rc(qr.at[7], g.at[pl.ds(4 * i, 4)], gS, gR.at[i], partner)

    odd_row = jnp.where(odd, x, xl)
    odd_other = jnp.where(odd, xo, xr)

    def row_sum(lev, p):
        t = (lev - 1) * 16 + p
        acc = us[ts[l, 0, t]] + ul[ts[leaf_of(xl), 0, t]]
        acc = acc + ur[ts[leaf_of(xr), 0, t]] + uo[ts[leaf_of(xo), 0, t]]
        return acc + v1a[ts[leaf_of(odd_row), 1, t]] + v1b[ts[leaf_of(odd_other), 1, t]]

    def quarters(k, with_l2):
        @pl.loop(0, 4)
        def _(i):
            p = 4 * x + i
            acc = row_sum(k + 3, p)
            if with_l2:
                acc = acc + v2r[ts[z * NX + 2, 1, (k + 2) * 16 + p]]
            qs[k, i] = acc

    def put_res(p, value):
        rows = pl.ds(pl.multiple_of(p * PAN, PAN), PAN)
        res[rows, :] = (srf[rows, :] - value).astype(BF16)

    def root_share():
        @pl.when(z == 1)
        def _():
            q_in(1).wait_recv()

            @pl.loop(0, 4)
            def _(i):
                qs[2, i] = qs[2, i] + qr[1, i]

        q_send(2).start()

    def collect(k, count, main):
        for i in range(count):
            q_in(i).wait_recv()

        @pl.loop(0, 4)
        def _(i):
            acc = qs[k, i]
            for s in range(count):
                acc = acc + qr[s, i]
            if main:
                g[i] = acc
            else:
                qr[7, i] = acc

        if main:
            for i in range(1, NX):
                g_in(i).wait_recv()
        else:
            g_send().start()

    width = swidth[l]

    @pl.loop(0, 5)
    def _(rnd):
        @pl.when(rnd == 0)
        def _():
            for j in range(8):
                send_a(j, 0).wait_recv()
                send_a(j, 1).wait_recv()
            fwd_b(0).start()
            fwd_b(1).start()

            @pl.when(level == 1)
            def _():
                @pl.loop(0, 16)
                def _(p):
                    put_res(p, us[ts[l, 0, p]] + ul[ts[leaf_of(xl), 0, p]])

        @pl.when(rnd == 1)
        def _():
            @pl.when(jnp.logical_not(odd))
            def _():
                for t in range(4):
                    v1_send(t, 0).wait_recv()
                    v1_send(t, 1).wait_recv()
                v1_fwd(0).start()
                v1_fwd(1).start()

            fwd_b(0).wait_recv()
            fwd_b(1).wait_recv()

            @pl.when(odd)
            def _():
                v1_fwd(0).wait_recv()
                v1_fwd(1).wait_recv()

            quarters(0, False)

            @pl.when(q_sends[0])
            def _():
                q_send(0).start()

            @pl.when(level == 2)
            def _():
                @pl.loop(0, 16)
                def _(p):
                    put_res(p, row_sum(2, p))

        @pl.when(rnd == 2)
        def _():
            @pl.when(jnp.logical_and(lax.rem(z, 2) == 1, x != 0))
            def _():
                collect(0, 1, False)

            @pl.when(x == 1)
            def _():
                for t in (0, 1, 2, 3):
                    v2_send(t, 0).wait_recv()
                    if t < 2:
                        v2_fwd(t).start()

            @pl.when(x == 3)
            def _():
                for t in (2, 3, 0, 1):
                    v2_send(t, 1).wait_recv()
                    if t >= 2:
                        v2_fwd(t).start()

            @pl.when(x == 0)
            def _():
                for t in (0, 2, 1, 3):
                    v2_fwd(t).wait_recv()

                    @pl.when(lax.rem(z, 2) == 0)
                    def _():
                        z_fwd(t).start()

            quarters(1, True)
            quarters(2, True)

            @pl.when(q_sends[1])
            def _():
                q_send(1).start()

            @pl.when(jnp.logical_and(q_sends[2], level != 3))
            def _():
                root_share()

            @pl.when(level == 3)
            def _():
                collect(0, 1, True)

            @pl.when(level == 3)
            def _():
                for t in range(4):
                    z_fwd(t).wait_recv()

                @pl.loop(0, 16)
                def _(p):
                    t = 2 * 16 + p
                    acc = g[p] + v2r[ts[z * NX + 2, 1, t]]
                    put_res(p, acc + v2p[ts[lax.rem(z + NZ - 1, NZ) * NX + 2, 1, t]])

        @pl.when(rnd == 3)
        def _():
            @pl.when(jnp.logical_and(zm == 2, x == 0))
            def _():
                collect(1, 3, True)

            @pl.when(jnp.logical_and(zm == 2, x != 0))
            def _():
                collect(1, 3, False)

            @pl.when(jnp.logical_and(z == 4, x == 0))
            def _():
                collect(2, 6, True)

            @pl.when(jnp.logical_and(z == 4, x != 0))
            def _():
                collect(2, 6, False)

            @pl.when(level == 4)
            def _():
                for i in range(2):
                    for t in range(4):
                        v3_in(i, t).wait_recv()

                @pl.loop(0, 16)
                def _(p):
                    t = 3 * 16 + p
                    acc = g[p] + v3[0, ts[lax.rem(z + NZ - 1, NZ) * NX, 1, t]]
                    put_res(p, acc + v3[1, ts[lax.rem(z + 1, NZ) * NX, 1, t]])

        @pl.when(rnd == 4)
        def _():
            @pl.when(first_relay)
            def _():
                for t in (0, 2, 1, 3):
                    e1(t, partner).wait_recv()
                    e2(t, at(x, 4)).start()

            @pl.when(last_relay)
            def _():
                for t in (0, 2, 1, 3):
                    e2(t, partner).wait_recv()
                    e3(t).start()

            @pl.when(level == 5)
            def _():
                for i in (1, 2):
                    v5_in(i).wait_recv()
                for i in range(2):
                    for t in range(4):
                        e3_in(i, t).wait_recv()
                for i in range(2):
                    for t in range(4):
                        v4_in(i, t).wait_recv()

                @pl.loop(0, 16)
                def _(p):
                    t = 4 * 16 + p
                    acc = g[p]
                    for i in range(4):
                        acc = acc + v3[i, ts[(2 * i + 1) * NX, 1, t]]
                    for i in range(2):
                        acc = acc + v4[i, ts[(4 * i + 2) * NX, 1, t]]
                    put_res(p, acc)

        @pl.when(level == rnd + 1)
        def _():
            for i in range(8):
                top = i * TILE
                y = mm(lf[top : top + TILE, : top + TILE], res[: top + TILE, :])
                rows = top + lax.broadcasted_iota(jnp.int32, (TILE, LANES), 0)
                yb[top : top + TILE, :] = jnp.where(rows < width, y, 0.0).astype(BF16)

            for t in (0, 2, 1, 3):
                @pl.when(level < 5)
                def _():
                    upd = mm(bf[t * TILE : (t + 1) * TILE, :], yb[...]).reshape(2, PAN, LANES)
                    w[2 * t : 2 * t + 2] = upd

                    @pl.when(level == 1)
                    def _():
                        v1a[2 * t : 2 * t + 2] = upd
                        v1_send(t, 0).start()
                        v1_send(t, 1).start()

                    @pl.when(level == 2)
                    def _():
                        v2r[2 * t : 2 * t + 2] = upd
                        v2_send(t, 0 if t < 2 else 1).start()

                    @pl.when(level == 3)
                    def _():
                        v3_send(t).start()

                    @pl.when(level == 4)
                    def _():
                        v4_send(t).start()

            @pl.when(level == 2)
            def _():
                for t in (2, 3):
                    v2_send(t, 0).start()
                for t in (0, 1):
                    v2_send(t, 1).start()

            @pl.when(jnp.logical_and(level == 3, far))
            def _():
                for t in (0, 2, 1, 3):
                    e1(t, at(side, z)).start()

            @pl.when(jnp.logical_and(level == 3, jnp.logical_not(far)))
            def _():
                v5_send().start()

            @pl.when(level == 3)
            def _():
                root_share()

    def yx():
        return rc(ysend, yrecv, yS, yR, partner)

    @pl.when(level > 0)
    def _():
        ysend[...] = yb[pl.ds(other, 1024), :].astype(F32)
        yx().start()
        mine = yb[pl.ds(half, 1024), :]
        yx().wait_recv()
        theirs = yrecv[...].astype(BF16)
        sout[:, :LANES] = jnp.where(first, mine, theirs)
        sout[:, LANES:] = jnp.where(first, theirs, mine)
        yx().wait_send()

    @pl.when(level == 0)
    def _():
        sout[...] = jnp.zeros_like(sout)

    @pl.when(c == 0)
    def _():
        for i in range(4):
            p10(i).wait_send()

    for j in range(8):
        ux(j).wait_send()
        send_a(j, 0).wait_send()
        send_a(j, 1).wait_send()
    for d in range(1, NX):
        tx(d).wait_send()
    for d in range(1, NZ):
        tz(d).wait_send()
    rx().wait_send()
    for j in range(8, 12):
        px(j).wait_send()
    fwd_b(0).wait_send()
    fwd_b(1).wait_send()

    @pl.when(odd)
    def _():
        for t in range(4):
            v1_send(t, 0).wait_send()
            v1_send(t, 1).wait_send()

    @pl.when(jnp.logical_not(odd))
    def _():
        v1_fwd(0).wait_send()
        v1_fwd(1).wait_send()

    @pl.when(x == 2)
    def _():
        for t in range(4):
            v2_send(t, 0).wait_send()
            v2_send(t, 1).wait_send()

    @pl.when(x == 1)
    def _():
        v2_fwd(0).wait_send()
        v2_fwd(1).wait_send()

    @pl.when(x == 3)
    def _():
        v2_fwd(2).wait_send()
        v2_fwd(3).wait_send()

    @pl.when(jnp.logical_and(x == 0, lax.rem(z, 2) == 0))
    def _():
        for t in range(4):
            z_fwd(t).wait_send()

    for k in range(3):
        @pl.when(q_sends[k])
        def _():
            q_send(k).wait_send()

    @pl.when(jnp.logical_and(x != 0, z != 0))
    def _():
        g_send().wait_send()

    @pl.when(level == 3)
    def _():
        for t in range(4):
            v3_send(t).wait_send()

    @pl.when(jnp.logical_and(level == 3, far))
    def _():
        for t in range(4):
            e1(t, at(side, z)).wait_send()

    @pl.when(jnp.logical_and(level == 3, jnp.logical_not(far)))
    def _():
        v5_send().wait_send()

    @pl.when(first_relay)
    def _():
        for t in range(4):
            e2(t, at(x, 4)).wait_send()

    @pl.when(last_relay)
    def _():
        for t in range(4):
            e3(t).wait_send()

    @pl.when(level == 4)
    def _():
        for t in range(4):
            v4_send(t).wait_send()


def on_device(
    leaf_rhs, leaf_inverse, leaf_below, leaf_rows,
    sep_rhs, sep_inverse, sep_below, sep_rows, sep_width,
):
    vmem = lambda *s, dtype=F32: pltpu.VMEM(s, dtype)
    dma = lambda *s: pltpu.SemaphoreType.DMA(s)
    pan = lambda *n: pltpu.VMEM((*n, PAN, LANES), F32)
    scratch = [
        vmem(2048, 1024, dtype=BF16),
        vmem(2048, 1024, dtype=BF16),
        vmem(1024, 256, dtype=BF16),
        vmem(1024, 256, dtype=BF16),
        vmem(2048, 2048, dtype=BF16),
        vmem(1024, 2048, dtype=BF16),
        vmem(4, 256, 1024),
        vmem(12, 256, 1024),
        pan(17), pan(17), pan(17), pan(17),
        pan(9), pan(9), pan(9), pan(9),
        pan(4, 9), pan(2, 9), pan(8),
        pan(3, 4), pan(8, 4), pan(16),
        vmem(4, 256, 256), vmem(4, 256, 256), vmem(256, 256),
        vmem(1024, 256, dtype=BF16),
        pan(8, 2), pan(8, 2),
        vmem(2048, 128), vmem(1024, 128),
        vmem(2048, 128, dtype=BF16), vmem(2048, 128, dtype=BF16),
        vmem(1024, 128), vmem(1024, 128),
        vmem(32, 8, 128, dtype=jnp.int32),
        pltpu.SMEM((32, 8, 128), jnp.int32),
        dma(7),
        dma(4), dma(4), dma(8), dma(8), dma(2, 8), dma(2, 8), dma(2), dma(2),
        dma(2, 4), dma(2, 4), dma(2), dma(2),
        dma(2, 4), dma(4), dma(2), dma(4), dma(4), dma(4),
        dma(4), dma(2, 4), pltpu.SemaphoreType.DMA, dma(4), dma(4), dma(2, 4),
        dma(3), dma(8), pltpu.SemaphoreType.DMA, dma(4), dma(12), dma(12),
        pltpu.SemaphoreType.DMA, pltpu.SemaphoreType.DMA,
        pltpu.SemaphoreType.DMA, pltpu.SemaphoreType.DMA,
        dma(3), dma(3), dma(7), dma(7), pltpu.SemaphoreType.DMA,
        dma(4), dma(4), dma(4), dma(4), dma(4), dma(2, 4),
    ]
    smem = pl.BlockSpec(memory_space=pltpu.SMEM)
    hbm = pl.BlockSpec(memory_space=pl.ANY)
    out = pl.BlockSpec(memory_space=pltpu.VMEM)
    return pl.pallas_call(
        kernel,
        out_shape=(
            jax.ShapeDtypeStruct((1024, 256), BF16),
            jax.ShapeDtypeStruct((1024, 256), BF16),
        ),
        in_specs=[smem, smem, smem, hbm, hbm, hbm, hbm, hbm, hbm],
        out_specs=(out, out),
        scratch_shapes=scratch,
        compiler_params=pltpu.CompilerParams(
            collective_id=0, has_side_effects=True, vmem_limit_bytes=66_000_000,
        ),
        name="forward_substitution",
    )(leaf_rows, sep_rows, sep_width, leaf_rhs, leaf_inverse, leaf_below, sep_rhs, sep_inverse, sep_below)


def solution(mesh):
    placed = (
        P(("leaf", "col"), "row"),
        P("leaf", "col"),
        P("leaf", "col"),
        P("leaf", None),
        P(("leaf", "col"), "row"),
        P("leaf", "col"),
        P("leaf", "col"),
        P("leaf", None),
        P(),
    )
    return jax.shard_map(
        on_device,
        mesh=mesh,
        in_specs=placed,
        out_specs=(P(("leaf", "col"), "row"), P(("leaf", "col"), "row")),
        check_vma=False,
    )
```
